32 devices in a mesh: rep: 4 (over z), col: 8 (over y, x, core).
Axes of the slice: x: 2, y: 2, z: 4, core: 2. Of those that a mesh axis runs over, the one named last changes fastest.
Arguments:
- acts: bfloat16 [8192, 4096], P('rep'), may hold values from -40 to 40
- cotangent: bfloat16 [8192, 8192], P('rep', 'col'), may hold values from -40 to 40
- weight: float32 [4096, 8192], P(('rep', 'col')), may hold values from -6 to 6
- moment: float32 [4096, 8192], P(('rep', 'col')), may hold values from -3 to 3
- second: float32 [4096, 8192], P(('rep', 'col')), may hold values from 0.25 to 4
Outputs:
- new_weight: float32 [4096, 8192], P(('rep', 'col'))
- new_moment: float32 [4096, 8192], P(('rep', 'col'))
- new_second: float32 [4096, 8192], P(('rep', 'col'))
- combined: float32 [4096, 8192], P(('rep', 'col'))
The draws below stay inside these ranges and needn't reach their ends.
All inputs are finite; a program needn't handle non-finite values.
Results may differ from the reference program's by a relative error of at most 0.0003.
Values may be sent and summed in bfloat16 or wider, within the bound.
No kernel may reach another device: no remote copies, remote signals or barrier semaphores. Data moves between devices by JAX's collectives and lax.ppermute only.
A program may use at most 128 MiB of HBM per device.

```python
import math
import jax
import jax.numpy as jnp

D = 4096
QW = 8192
TOK_DEV = 2048
REPS = 4
N_REP = 4


def block_weights(key, width):
    levels = jnp.exp(jax.random.uniform(key, (REPS, 16), jnp.float32, math.log(0.2), math.log(2.0)))
    spread = jnp.broadcast_to(levels[:, :, None], (REPS, 16, width // 16))
    return spread.reshape(REPS, width)


def draw_acts(key, part):
    keys = jax.random.split(key, 4)
    row_weights = block_weights(keys[3], D)
    common = jnp.clip(jax.random.normal(keys[0], (TOK_DEV, D), jnp.float32), -5.0, 5.0)
    noise = jnp.clip(jax.random.normal(keys[1], (REPS, TOK_DEV, D), jnp.float32), -5.0, 5.0)
    mixed = row_weights[:, None, :] * common[None] + 0.6 * noise
    scales = 0.3 * jnp.exp(jax.random.uniform(keys[2], (D,), jnp.float32, 0.0, math.log(10.0)))
    return (mixed * scales).reshape(REPS * TOK_DEV, D).astype(jnp.bfloat16)


def draw_cotangent(key, part):
    keys = jax.random.split(key, 4)
    column_weights = block_weights(keys[3], QW)
    common = jnp.clip(jax.random.normal(keys[0], (TOK_DEV, QW), jnp.float32), -5.0, 5.0)
    noise = jnp.clip(jax.random.normal(keys[1], (REPS, TOK_DEV, QW), jnp.float32), -5.0, 5.0)
    mixed = column_weights[:, None, :] * common[None] + noise
    trend = jnp.exp(math.log(3.0) * jnp.arange(QW, dtype=jnp.float32) / QW)
    rough = jnp.exp(jax.random.uniform(keys[2], (QW,), jnp.float32, -0.7, 0.7))
    values = mixed * (trend * rough) / math.sqrt(TOK_DEV)
    return values.reshape(REPS * TOK_DEV, QW).astype(jnp.bfloat16)


def shard_levels(own_key, shape, pieces, low, largest):
    gain = 1.0
    for axis_at, shards_of in pieces:
        heights = jax.random.uniform(jax.random.fold_in(jax.random.fold_in(own_key, 6), axis_at), (shards_of,), jnp.float32, low / len(pieces), largest / len(pieces))
        gain = gain * jnp.repeat(jnp.exp(heights), shape[axis_at] // shards_of).reshape((-1,) + (1,) * (len(shape) - 1 - axis_at))
    return gain


def centred(rng, extent, scale, reach, cuts=(), kind=jnp.bfloat16):
    result = scale * jax.random.normal(rng, extent, jnp.float32)
    if cuts:
        result = result * shard_levels(rng, extent, cuts, -0.22, 0.18)
    return jnp.clip(result, -reach, reach).astype(kind)


def setup_inputs(seed: int = 0) -> dict:
    streams_of = jax.random.split(jax.random.key(seed), 6)
    acts = draw_acts(jax.random.fold_in(streams_of[5], 71), 0)
    cotangent = draw_cotangent(jax.random.fold_in(streams_of[5], 71), 0)
    weight = centred(streams_of[2], (D, QW), 1.0, 6.0, ((0, 32),), jnp.float32)
    moment = centred(streams_of[3], (D, QW), 0.5, 3.0, ((0, 32),), jnp.float32)
    second = jnp.clip(jnp.exp(math.log(4.0) - 2.7725887 * jax.random.uniform(streams_of[4], (D, QW), jnp.float32) ** shard_levels(streams_of[4], (D, QW), ((0, 32),), -0.2, 0.2)), 0.25, 4.0)
    return dict(acts=acts, cotangent=cotangent, weight=weight, moment=moment, second=second)


bias_first = 0.9999734386011124
bias_second = 0.99407947077966

def adasum_pair(first, later):
    cross = jnp.sum(first * later)
    first_sq = jnp.sum(first * first)
    later_sq = jnp.sum(later * later)
    return (1.0 - cross / (2.0 * (first_sq + 1e-06))) * first + (1.0 - cross / (2.0 * (later_sq + 1e-06))) * later

def reference(acts, cotangent, weight, moment, second):
    inputs = acts.reshape(N_REP, TOK_DEV, D)
    outgrad = cotangent.reshape(N_REP, TOK_DEV, QW)
    vectors = [jnp.dot(inputs[r].T, outgrad[r], preferred_element_type=jnp.float32) for r in range(N_REP)]
    while len(vectors) > 1:
        vectors = [adasum_pair(vectors[2 * j], vectors[2 * j + 1]) for j in range(len(vectors) // 2)]
    combined = vectors[0]
    new_moment = 0.9 * moment + 0.1 * combined
    new_second = 0.95 * second + 0.05 * combined * combined
    update = new_moment / bias_first / (jnp.sqrt(new_second / bias_second) + 1e-08) + 0.1 * weight
    new_weight = weight - 0.0003 * update
    return (new_weight, new_moment, new_second, combined)
```

```python
import jax
import jax.numpy as jnp
from jax import lax
from jax.experimental import pallas as pl
from jax.experimental.pallas import tpu as pltpu
from jax.sharding import PartitionSpec as P

bias_first = 0.9999734386011124
bias_second = 0.99407947077966


TOP = 2.0**7.875
TINY = 1e-30


def peer(rank, step, count):
    if count & (count - 1) == 0:
        return rank ^ step
    return (step - rank) % count


def chosen(rank, count):
    peers = jnp.stack([peer(rank, step, count) for step in range(count)])
    return peers[:, None] == jnp.arange(count)[None, :]


def encode(block, largest):
    unit = jnp.abs(block) * (TOP / jnp.maximum(largest, TINY))
    power = unit * unit
    power = power * power
    power = power * power
    power = power * power
    return jnp.where(block < 0, -power, power).astype(jnp.bfloat16)


def decode(code):
    code = code.astype(jnp.float32)
    unit = jnp.exp2(jnp.log2(jnp.abs(code)) * (1.0 / 16.0))
    return jnp.where(code < 0, -unit, unit)


def gradient_kernel(count, *refs):
    table, acts, cotangent = refs[0], refs[1 : 1 + count], refs[1 + count]
    codes, tops = refs[2 + count : 2 + 2 * count], refs[2 + 2 * count]
    rows = acts[0].shape[1]
    left = jnp.concatenate([ref[...] for ref in acts], axis=1)
    gradient = lax.dot_general(
        left, cotangent[...], (((0,), (0,)), ((), ())), preferred_element_type=jnp.float32
    )
    for at in range(count):
        block = gradient[at * rows : (at + 1) * rows]
        largest = jnp.max(jnp.abs(block), keepdims=True)
        codes[at][...] = encode(block, largest)
        tops[at : at + 1, :] = jnp.broadcast_to(largest, (1, tops.shape[1]))


def gradient_tiles(acts, cotangent, blocks, rows):
    tokens, columns = cotangent.shape
    count = len(blocks)
    tile = jax.ShapeDtypeStruct((rows, columns), jnp.bfloat16)
    if rows % 128:
        codes, tops = [], []
        for block in blocks:
            left = lax.dynamic_slice_in_dim(acts, block * rows, rows, 1)
            part = jnp.einsum("td,tc->dc", left, cotangent, preferred_element_type=jnp.float32)
            tops.append(jnp.max(jnp.abs(part)))
            codes.append(encode(part, tops[-1]))
        return codes, jnp.stack(tops)

    def block_of(at):
        return pl.BlockSpec((tokens, rows), lambda i, table: (0, table[at]))

    outs = pl.pallas_call(
        lambda *refs: gradient_kernel(count, *refs),
        out_shape=[tile] * count + [jax.ShapeDtypeStruct((count, 128), jnp.float32)],
        grid_spec=pltpu.PrefetchScalarGridSpec(
            num_scalar_prefetch=1,
            grid=(1,),
            in_specs=[block_of(at) for at in range(count)]
            + [pl.BlockSpec((tokens, columns), lambda i, table: (0, 0))],
            out_specs=[pl.BlockSpec((rows, columns), lambda i, table: (0, 0))] * count
            + [pl.BlockSpec((count, 128), lambda i, table: (0, 0))],
        ),
        cost_estimate=pl.CostEstimate(
            flops=2 * tokens * rows * columns * count,
            bytes_accessed=2 * tokens * (rows * count + columns) + 2 * rows * columns * count,
            transcendentals=0,
        ),
        name="gradient",
    )(jnp.stack(blocks).astype(jnp.int32), *([acts] * count), cotangent)
    return outs[:count], outs[count][:, 0]


def pairs_of(count):
    return [(a, b) for a in range(count) for b in range(a, count)]


def gram_kernel(count, table, *refs):
    codes = refs[:count]
    units, sums = refs[-2], refs[-1]
    rows, columns = codes[0].shape
    step = 16
    pairs = pairs_of(count)

    def body(at, carry):
        carry = list(carry)
        window = pl.ds(pl.multiple_of(at * step, step), step)
        for column in range(0, columns, 128):
            lanes = slice(column, column + 128)
            values = [decode(ref[window, lanes]) for ref in codes]
            for replica, value in enumerate(values):
                units[replica, window, lanes] = value
            for index, (a, b) in enumerate(pairs):
                carry[index] = carry[index] + values[a] * values[b]
        return tuple(carry)

    zero = jnp.zeros((step, 128), jnp.float32)
    carry = lax.fori_loop(0, rows // step, body, (zero,) * len(pairs))
    for index, value in enumerate(carry):
        sums[index : index + 1, :] = jnp.sum(value, axis=0, keepdims=True)


def gram_tiles(codes, units, place, shape):
    count = len(codes)
    rows, columns = codes[0].shape
    pairs = len(pairs_of(count))
    tile = pl.BlockSpec((rows, columns), lambda i, table: (0, 0))
    first = units is None
    return pl.pallas_call(
        lambda *refs: gram_kernel(count, *refs),
        out_shape=[
            jax.ShapeDtypeStruct(shape, jnp.float32),
            jax.ShapeDtypeStruct((pairs, 128), jnp.float32),
        ],
        grid_spec=pltpu.PrefetchScalarGridSpec(
            num_scalar_prefetch=1,
            grid=(1,),
            in_specs=[tile] * count + ([] if first else [pl.BlockSpec(memory_space=pl.ANY)]),
            out_specs=[
                pl.BlockSpec((count, rows, columns), lambda i, table: (0, 0, table[0])),
                pl.BlockSpec((pairs, 128), lambda i, table: (0, 0)),
            ],
        ),
        input_output_aliases={} if first else {count + 1: 0},
        cost_estimate=pl.CostEstimate(
            flops=rows * columns * (2 * pairs + 10 * count),
            bytes_accessed=6 * rows * columns * count,
            transcendentals=2 * rows * columns * count,
        ),
        name="gram",
    )(jnp.stack([place]).astype(jnp.int32), *codes, *([] if first else [units]))


def update_kernel(count, coefs, units, weight, moment, second, *outs):
    new_weight, new_moment, new_second, combined = outs
    here = pl.program_id(0)
    total = units[0] * coefs[0, here]
    for replica in range(1, count):
        total = total + units[replica] * coefs[replica, here]
    combined[...] = total
    first = 0.9 * moment[...] + 0.1 * total
    square = 0.95 * second[...] + 0.05 * total * total
    new_moment[...] = first
    new_second[...] = square
    update = first / bias_first / (jnp.sqrt(square / bias_second) + 1e-08) + 0.1 * weight[...]
    new_weight[...] = weight[...] - 0.0003 * update


def update_rows(units, coefs, weight, moment, second, columns):
    count, rows, width = units.shape
    block = pl.BlockSpec((rows, columns), lambda i: (0, i))
    return pl.pallas_call(
        lambda *refs: update_kernel(count, *refs),
        out_shape=[jax.ShapeDtypeStruct((rows, width), jnp.float32)] * 4,
        grid=(width // columns,),
        in_specs=[
            pl.BlockSpec(memory_space=pltpu.SMEM),
            pl.BlockSpec((count, rows, columns), lambda i: (0, 0, i)),
            block,
            block,
            block,
        ],
        out_specs=[block] * 4,
        name="update",
    )(coefs, units, weight, moment, second)


def replica_weights(gram, levels):
    count = gram.shape[0]
    vectors = [jnp.where(jnp.arange(count) == r, 1.0, 0.0) for r in range(count)]

    def inner(a, b):
        return jnp.sum(a[:, None] * b[None, :] * gram)

    for level in range(levels):
        merged = []
        for at in range(0, len(vectors), 2):
            a, b = vectors[at], vectors[at + 1]
            cross = inner(a, b)
            a_coef = 1.0 - cross / (2.0 * (inner(a, a) + 1e-06))
            b_coef = 1.0 - cross / (2.0 * (inner(b, b) + 1e-06))
            merged.append(a_coef * a + b_coef * b)
        vectors = merged
    return vectors[0]


def per_device(acts, cotangent, weight, moment, second):
    replicas, shards = lax.axis_size("rep"), lax.axis_size("col")
    rep_rank, col_rank = lax.axis_index("rep"), lax.axis_index("col")
    levels = replicas.bit_length() - 1
    rows, width = weight.shape
    columns = cotangent.shape[1]

    def sent(block, rep_step, col_step):
        route = []
        for r in range(replicas):
            for c in range(shards):
                target = peer(r, rep_step, replicas) * shards + peer(c, col_step, shards)
                route.append((r * shards + c, target))
        return lax.ppermute(block, ("rep", "col"), route)

    received, tops = [], []
    for col_step in range(shards):
        col_peer = peer(col_rank, col_step, shards)
        blocks = [peer(rep_rank, s, replicas) * shards + col_peer for s in range(replicas)]
        codes, group_tops = gradient_tiles(acts, cotangent, blocks, rows)
        tops.append(group_tops)
        arrived = list(codes)
        for rep_step in sorted(range(replicas), key=lambda s: (s < replicas // 2, s)):
            if rep_step or col_step:
                arrived[rep_step] = sent(codes[rep_step], rep_step, col_step)
        received.append(arrived)

    rel = jnp.stack(tops)
    col_hot = chosen(col_rank, shards)
    rep_hot = chosen(rep_rank, replicas)
    by_target = jnp.sum(
        jnp.where(rep_hot[None, :, :, None] & col_hot[:, None, None, :], rel[:, :, None, None], 0.0),
        axis=(0, 1),
    )
    wide = jnp.broadcast_to(by_target.reshape(-1, 1), (replicas * shards, 128))
    scales = lax.all_to_all(wide, ("rep", "col"), 0, 0, tiled=True)[:, 0]
    scales = scales.reshape(replicas, shards) * (1.0 / TOP)
    step_scales = jnp.sum(
        jnp.where(rep_hot[None, :, :, None] & col_hot[:, None, None, :], scales[None, None], 0.0),
        axis=(2, 3),
    )

    units, sums = None, []
    for col_step in range(shards):
        place = peer(col_rank, col_step, shards)
        units, part = gram_tiles(received[col_step], units, place, (replicas, rows, width))
        sums.append(part)
    totals = jnp.sum(jnp.stack(sums), axis=2)
    partial = []
    lookup = {pair: i for i, pair in enumerate(pairs_of(replicas))}
    for a in range(replicas):
        for b in range(replicas):
            products = totals[:, lookup[(min(a, b), max(a, b))]]
            partial.append(jnp.sum(products * step_scales[:, a] * step_scales[:, b]))
    by_step = jnp.stack(partial).reshape(replicas, replicas)
    by_replica = jnp.sum(
        jnp.where(rep_hot[:, None, :, None] & rep_hot[None, :, None, :], by_step[:, :, None, None], 0.0),
        axis=(0, 1),
    )
    flat = jnp.pad(by_replica.reshape(1, -1), ((0, 0), (0, 128 - replicas * replicas)))
    wide = jnp.broadcast_to(flat, (replicas * shards, 128))
    gram = jnp.sum(lax.all_to_all(wide, ("rep", "col"), 0, 0, tiled=True), axis=0)
    gram = gram[: replicas * replicas].reshape(replicas, replicas)
    weights = replica_weights(gram, levels)
    step_weights = jnp.sum(jnp.where(rep_hot, weights[None, :], 0.0), axis=1)
    by_shard = jnp.sum(jnp.where(rep_hot[:, :, None], scales[None], 0.0), axis=1)
    coefs = step_weights[:, None] * by_shard
    return tuple(update_rows(units, coefs, weight, moment, second, columns))


def solution(mesh):
    return jax.shard_map(
        per_device,
        mesh=mesh,
        in_specs=(
            P("rep", None),
            P("rep", "col"),
            P(("rep", "col"), None),
            P(("rep", "col"), None),
            P(("rep", "col"), None),
        ),
        out_specs=(
            P(("rep", "col"), None),
            P(("rep", "col"), None),
            P(("rep", "col"), None),
            P(("rep", "col"), None),
        ),
        check_vma=False,
    )
```

```python
import jax
import jax.numpy as jnp
from jax import lax
from jax.experimental import pallas as pl
from jax.experimental.pallas import tpu as pltpu
from jax.sharding import PartitionSpec as P

bias_first = 0.9999734386011124
bias_second = 0.99407947077966


TOP = 2.0**7.875
TINY = 1e-30
LANES, PAD = 128, 16


def peer(rank, step, count):
    if count & (count - 1) == 0:
        return rank ^ step
    return (step - rank) % count


def encode(block, largest):
    unit = jnp.abs(block) * (TOP / jnp.maximum(largest, TINY))
    power = unit * unit
    power = power * power
    power = power * power
    power = power * power
    return jnp.where(block < 0, -power, power).astype(jnp.bfloat16)


def decode(code, scale):
    code = code.astype(jnp.float32)
    unit = jnp.exp2(jnp.log2(jnp.abs(code)) * (1.0 / 16.0)) * scale
    return jnp.where(code < 0, -unit, unit)


def scale_of(block):
    largest = jnp.max(jnp.abs(block), keepdims=True) * (1.0 + 2.0**-7)
    return largest.astype(jnp.bfloat16)


def packed_shape(rows, columns):
    return (rows * columns // LANES + PAD, LANES)


def gradient_kernel(count, *refs):
    acts, cotangent, codes = refs[1 : 1 + count], refs[1 + count], refs[2 + count :]
    rows, columns = acts[0].shape[1], cotangent.shape[1]
    left = jnp.concatenate([ref[...] for ref in acts], axis=1)
    gradient = lax.dot_general(
        left, cotangent[...], (((0,), (0,)), ((), ())), preferred_element_type=jnp.float32
    )
    for at in range(count):
        block = gradient[at * rows : (at + 1) * rows]
        largest = scale_of(block)
        code = encode(block, largest.astype(jnp.float32))
        for part in range(columns // LANES):
            lanes = slice(part * LANES, (part + 1) * LANES)
            codes[at][part * rows : (part + 1) * rows, :] = code[:, lanes]
        codes[at][rows * columns // LANES :, :] = jnp.broadcast_to(largest, (PAD, LANES))


def gradient_tiles(acts, cotangent, blocks, rows):
    tokens, columns = cotangent.shape
    count = len(blocks)
    packed = packed_shape(rows, columns)
    if rows % LANES:
        codes = []
        for block in blocks:
            left = lax.dynamic_slice_in_dim(acts, block * rows, rows, 1)
            part = jnp.einsum("td,tc->dc", left, cotangent, preferred_element_type=jnp.float32)
            largest = scale_of(part)
            code = encode(part, largest.astype(jnp.float32))
            code = code.reshape(rows, -1, LANES).transpose(1, 0, 2).reshape(-1, LANES)
            codes.append(jnp.concatenate([code, jnp.broadcast_to(largest, (PAD, LANES))]))
        return codes

    def block_of(at):
        return pl.BlockSpec((tokens, rows), lambda i, table: (0, table[at]))

    return pl.pallas_call(
        lambda *refs: gradient_kernel(count, *refs),
        out_shape=[jax.ShapeDtypeStruct(packed, jnp.bfloat16)] * count,
        grid_spec=pltpu.PrefetchScalarGridSpec(
            num_scalar_prefetch=1,
            grid=(1,),
            in_specs=[block_of(at) for at in range(count)]
            + [pl.BlockSpec((tokens, columns), lambda i, table: (0, 0))],
            out_specs=[pl.BlockSpec(packed, lambda i, table: (0, 0))] * count,
        ),
        cost_estimate=pl.CostEstimate(
            flops=2 * tokens * rows * columns * count,
            bytes_accessed=2 * tokens * (rows * count + columns) + 2 * rows * columns * count,
            transcendentals=0,
        ),
        name="gradient",
    )(jnp.stack(blocks).astype(jnp.int32), *([acts] * count), cotangent)


def pairs_of(count):
    return [(a, b) for a in range(count) for b in range(a, count)]


def gram_kernel(count, first, table, *refs):
    codes = refs[:count]
    units, sums = refs[-2], refs[-1]
    rows, columns = units.shape[1:]
    pairs = pairs_of(count)
    scales = [ref[-PAD:, :].astype(jnp.float32) * (1.0 / TOP) for ref in codes]

    def body(at, carry):
        carry = list(carry)
        row = pl.multiple_of(at * PAD, PAD)
        for part in range(columns // LANES):
            lanes = slice(part * LANES, (part + 1) * LANES)
            values = [
                decode(ref[pl.ds(part * rows + row, PAD), :], scale)
                for ref, scale in zip(codes, scales)
            ]
            for replica, value in enumerate(values):
                units[replica, pl.ds(row, PAD), lanes] = value
            for index, (a, b) in enumerate(pairs):
                carry[index] = carry[index] + values[a] * values[b]
        return tuple(carry)

    zero = jnp.zeros((PAD, LANES), jnp.float32)
    carry = lax.fori_loop(0, rows // PAD, body, (zero,) * len(pairs))
    lane = lax.broadcasted_iota(jnp.int32, (8, sums.shape[1]), 1)
    total = jnp.zeros((8, sums.shape[1]), jnp.float32) if first else refs[count + 1][...]
    for value, (a, b) in zip(carry, pairs):
        value = jnp.sum(value, keepdims=True)
        here = lane == table[1 + a] * count + table[1 + b]
        here = here | (lane == table[1 + b] * count + table[1 + a])
        total = total + jnp.where(here, value, 0.0)
    sums[...] = jnp.concatenate([total] * (sums.shape[0] // 8), axis=0)


def gram_tiles(codes, before, place, order, shape, devices):
    count, rows, width = shape
    packed = codes[0].shape
    columns = (packed[0] - PAD) * LANES // rows
    wide = -(-count * count // LANES) * LANES
    first = before is None
    extra = [] if first else [pl.BlockSpec(memory_space=pl.ANY), pl.BlockSpec((8, wide), lambda i, table: (0, 0))]
    return pl.pallas_call(
        lambda *refs: gram_kernel(count, first, *refs),
        out_shape=[
            jax.ShapeDtypeStruct(shape, jnp.float32),
            jax.ShapeDtypeStruct((devices * 8, wide), jnp.float32),
        ],
        grid_spec=pltpu.PrefetchScalarGridSpec(
            num_scalar_prefetch=1,
            grid=(1,),
            in_specs=[pl.BlockSpec(packed, lambda i, table: (0, 0))] * count + extra,
            out_specs=[
                pl.BlockSpec((count, rows, columns), lambda i, table: (0, 0, table[0])),
                pl.BlockSpec((devices * 8, wide), lambda i, table: (0, 0)),
            ],
        ),
        input_output_aliases={} if first else {count + 1: 0},
        cost_estimate=pl.CostEstimate(
            flops=rows * columns * (2 * len(pairs_of(count)) + 10 * count),
            bytes_accessed=6 * rows * columns * count,
            transcendentals=2 * rows * columns * count,
        ),
        name="gram",
    )(jnp.stack([place] + order).astype(jnp.int32), *codes, *([] if first else before))


def replica_weights(inner, count):
    vectors = [[1.0 if r == s else 0.0 for s in range(count)] for r in range(count)]

    def product(a, b):
        total = 0.0
        for r in range(count):
            for s in range(count):
                if not zero(a[r]) and not zero(b[s]):
                    total = total + a[r] * b[s] * inner[r][s]
        return total

    while len(vectors) > 1:
        merged = []
        for at in range(0, len(vectors), 2):
            a, b = vectors[at], vectors[at + 1]
            cross = product(a, b)
            a_coef = 1.0 - cross / (2.0 * (product(a, a) + 1e-06))
            b_coef = 1.0 - cross / (2.0 * (product(b, b) + 1e-06))
            merged.append([scaled(b_coef, y) if zero(x) else scaled(a_coef, x) for x, y in zip(a, b)])
        vectors = merged
    return vectors[0]


def zero(value):
    return isinstance(value, float) and value == 0.0


def scaled(coef, value):
    return 0.0 if zero(value) else coef * value


def update_kernel(count, table, gathered, units, weight, moment, second, *outs):
    new_weight, new_moment, new_second, combined, coefs = outs

    @pl.when(pl.program_id(0) == 0)
    def _():
        total = jnp.sum(gathered[...], axis=0, keepdims=True) * 0.125
        lane = lax.broadcasted_iota(jnp.int32, total.shape, 1)

        def entry(r, s):
            at = min(r, s) * count + max(r, s)
            return jnp.sum(jnp.where(lane == at, total, 0.0), axis=1, keepdims=True)

        inner = [[entry(r, s) for s in range(count)] for r in range(count)]
        weights = replica_weights(inner, count)
        for step in range(count):
            value = jnp.zeros((1, 1), jnp.float32)
            for replica in range(count):
                value = jnp.where(table[step] == replica, weights[replica], value)
            coefs[step : step + 1, :] = jnp.broadcast_to(value, (1, LANES))

    total = units[0] * coefs[0:1, 0:1]
    for step in range(1, count):
        total = total + units[step] * coefs[step : step + 1, 0:1]
    combined[...] = total
    first = 0.9 * moment[...] + 0.1 * total
    square = 0.95 * second[...] + 0.05 * total * total
    new_moment[...] = first
    new_second[...] = square
    root = jnp.sqrt(square * (1.0 / bias_second)) + 1e-08
    update = first * (1.0 / bias_first) / root + 0.1 * weight[...]
    new_weight[...] = weight[...] - 0.0003 * update


def update_rows(gathered, units, weight, moment, second, order, columns):
    count, rows, width = units.shape
    block = pl.BlockSpec((rows, columns), lambda i, table: (0, i))
    return pl.pallas_call(
        lambda *refs: update_kernel(count, *refs),
        out_shape=[jax.ShapeDtypeStruct((rows, width), jnp.float32)] * 4,
        grid_spec=pltpu.PrefetchScalarGridSpec(
            num_scalar_prefetch=1,
            grid=(width // columns,),
            in_specs=[
                pl.BlockSpec(gathered.shape, lambda i, table: (0, 0)),
                pl.BlockSpec((count, rows, columns), lambda i, table: (0, 0, i)),
                block,
                block,
                block,
            ],
            out_specs=[block] * 4,
            scratch_shapes=[pltpu.VMEM((max(count, 8), LANES), jnp.float32)],
        ),
        name="update",
    )(jnp.stack(order).astype(jnp.int32), gathered, units, weight, moment, second)


def per_device(acts, cotangent, weight, moment, second):
    replicas, shards = lax.axis_size("rep"), lax.axis_size("col")
    rep_rank, col_rank = lax.axis_index("rep"), lax.axis_index("col")
    devices = replicas * shards
    rows, width = weight.shape
    columns = cotangent.shape[1]
    rep_peers = [peer(rep_rank, step, replicas) for step in range(replicas)]
    col_peers = [peer(col_rank, step, shards) for step in range(shards)]

    def sent(block, rep_step, col_step):
        route = []
        for r in range(replicas):
            for c in range(shards):
                target = peer(r, rep_step, replicas) * shards + peer(c, col_step, shards)
                route.append((r * shards + c, target))
        return lax.ppermute(block, ("rep", "col"), route)

    far_first = sorted(range(replicas), key=lambda step: (step < replicas // 2, -step))
    half = replicas // 2
    received = {}
    for col_step in range(shards):
        runs = [far_first[:half], far_first[half:]] if col_step == 0 else [far_first]
        for run in runs:
            blocks = [rep_peers[step] * shards + col_peers[col_step] for step in run]
            codes = gradient_tiles(acts, cotangent, blocks, rows)
            for rep_step, code in zip(run, codes):
                if rep_step or col_step:
                    code = sent(code, rep_step, col_step)
                received[rep_step, col_step] = code

    state = None
    for col_step in range(shards):
        codes = [received[step, col_step] for step in range(replicas)]
        shape = (replicas, rows, width)
        state = gram_tiles(codes, state, col_peers[col_step], rep_peers, shape, devices)
    units, sums = state
    gathered = lax.all_to_all(sums, ("rep", "col"), 0, 0, tiled=True)
    return tuple(update_rows(gathered, units, weight, moment, second, rep_peers, columns))


def solution(mesh):
    return jax.shard_map(
        per_device,
        mesh=mesh,
        in_specs=(
            P("rep", None),
            P("rep", "col"),
            P(("rep", "col"), None),
            P(("rep", "col"), None),
            P(("rep", "col"), None),
        ),
        out_specs=(
            P(("rep", "col"), None),
            P(("rep", "col"), None),
            P(("rep", "col"), None),
            P(("rep", "col"), None),
        ),
        check_vma=False,
    )
```

```python
import jax
import jax.numpy as jnp
from jax import lax
from jax.experimental import pallas as pl
from jax.experimental.pallas import tpu as pltpu
from jax.sharding import PartitionSpec as P

bias_first = 0.9999734386011124
bias_second = 0.99407947077966


TOP = 2.0**7.875
TINY = 1e-30
LANES, PAD = 128, 16


def peer(rank, step, count):
    if count & (count - 1) == 0:
        return rank ^ step
    return (step - rank) % count


def encode(block, largest):
    unit = jnp.abs(block) * (TOP / jnp.maximum(largest, TINY))
    power = unit * unit
    power = power * power
    power = power * power
    power = power * power
    return jnp.where(block < 0, -power, power).astype(jnp.bfloat16)


def decode(code, scale):
    code = code.astype(jnp.float32)
    unit = jnp.exp2(jnp.log2(jnp.abs(code)) * (1.0 / 16.0)) * scale
    return jnp.where(code < 0, -unit, unit)


def scale_of(block):
    largest = jnp.max(jnp.abs(block), keepdims=True) * (1.0 + 2.0**-7)
    return largest.astype(jnp.bfloat16)


def packed_shape(rows, columns):
    return (rows * columns // LANES + PAD, LANES)


def gradient_kernel(count, *refs):
    acts, cotangent, codes = refs[1 : 1 + count], refs[1 + count], refs[2 + count :]
    rows, columns = acts[0].shape[1], cotangent.shape[1]
    left = jnp.concatenate([ref[...] for ref in acts], axis=1)
    gradient = lax.dot_general(
        left, cotangent[...], (((0,), (0,)), ((), ())), preferred_element_type=jnp.float32
    )
    for at in range(count):
        block = gradient[at * rows : (at + 1) * rows]
        largest = scale_of(block)
        code = encode(block, largest.astype(jnp.float32))
        for part in range(columns // LANES):
            lanes = slice(part * LANES, (part + 1) * LANES)
            codes[at][part * rows : (part + 1) * rows, :] = code[:, lanes]
        codes[at][rows * columns // LANES :, :] = jnp.broadcast_to(largest, (PAD, LANES))


def gradient_tiles(acts, cotangent, table, block, count, rows):
    tokens, columns = cotangent.shape
    packed = packed_shape(rows, columns)
    if rows % LANES:
        codes = []
        for at in range(count):
            left = lax.dynamic_slice_in_dim(acts, block(table, at) * rows, rows, 1)
            part = jnp.einsum("td,tc->dc", left, cotangent, preferred_element_type=jnp.float32)
            largest = scale_of(part)
            code = encode(part, largest.astype(jnp.float32))
            code = code.reshape(rows, -1, LANES).transpose(1, 0, 2).reshape(-1, LANES)
            codes.append(jnp.concatenate([code, jnp.broadcast_to(largest, (PAD, LANES))]))
        return codes

    def block_of(at):
        return pl.BlockSpec((tokens, rows), lambda i, table: (0, block(table, at)))

    return pl.pallas_call(
        lambda *refs: gradient_kernel(count, *refs),
        out_shape=[jax.ShapeDtypeStruct(packed, jnp.bfloat16)] * count,
        grid_spec=pltpu.PrefetchScalarGridSpec(
            num_scalar_prefetch=1,
            grid=(1,),
            in_specs=[block_of(at) for at in range(count)]
            + [pl.BlockSpec((tokens, columns), lambda i, table: (0, 0))],
            out_specs=[pl.BlockSpec(packed, lambda i, table: (0, 0))] * count,
        ),
        cost_estimate=pl.CostEstimate(
            flops=2 * tokens * rows * columns * count,
            bytes_accessed=2 * tokens * (rows * count + columns) + 2 * rows * columns * count,
            transcendentals=0,
        ),
        name="gradient",
    )(table, *([acts] * count), cotangent)


def pairs_of(count):
    return [(a, b) for a in range(count) for b in range(a, count)]


def gram_kernel(count, step, first, table, *refs):
    codes = refs[:count]
    units, sums = refs[-2], refs[-1]
    rows = units.shape[1]
    columns = (codes[0].shape[0] - PAD) * LANES // rows
    left = pl.multiple_of(table[count + step] * columns, LANES)
    pairs = pairs_of(count)
    scales = [ref[-PAD:, :].astype(jnp.float32) * (1.0 / TOP) for ref in codes]

    def body(at, carry):
        carry = list(carry)
        row = pl.multiple_of(at * PAD, PAD)
        for part in range(columns // LANES):
            values = [
                decode(ref[pl.ds(part * rows + row, PAD), :], scale)
                for ref, scale in zip(codes, scales)
            ]
            for replica, value in enumerate(values):
                units[replica, pl.ds(row, PAD), pl.ds(left + part * LANES, LANES)] = value
            for index, (a, b) in enumerate(pairs):
                carry[index] = carry[index] + values[a] * values[b]
        return tuple(carry)

    zero = jnp.zeros((PAD, LANES), jnp.float32)
    carry = lax.fori_loop(0, rows // PAD, body, (zero,) * len(pairs))
    lane = lax.broadcasted_iota(jnp.int32, (8, sums.shape[1]), 1)
    total = jnp.zeros((8, sums.shape[1]), jnp.float32) if first else refs[count + 1][...]
    for value, (a, b) in zip(carry, pairs):
        value = jnp.sum(value, keepdims=True)
        here = lane == table[a] * count + table[b]
        here = here | (lane == table[b] * count + table[a])
        total = total + jnp.where(here, value, 0.0)
    sums[...] = jnp.concatenate([total] * (sums.shape[0] // 8), axis=0)


def gram_tiles(codes, before, table, step, shape, devices):
    count, rows, width = shape
    packed = codes[0].shape
    columns = (packed[0] - PAD) * LANES // rows
    wide = -(-count * count // LANES) * LANES
    first = before is None
    extra = [] if first else [pl.BlockSpec(memory_space=pltpu.VMEM), pl.BlockSpec((8, wide), lambda i, table: (0, 0))]
    return pl.pallas_call(
        lambda *refs: gram_kernel(count, step, first, *refs),
        out_shape=[
            jax.ShapeDtypeStruct(shape, jnp.float32),
            jax.ShapeDtypeStruct((devices * 8, wide), jnp.float32),
        ],
        grid_spec=pltpu.PrefetchScalarGridSpec(
            num_scalar_prefetch=1,
            grid=(1,),
            in_specs=[pl.BlockSpec(packed, lambda i, table: (0, 0))] * count + extra,
            out_specs=[
                pl.BlockSpec(memory_space=pltpu.VMEM),
                pl.BlockSpec((devices * 8, wide), lambda i, table: (0, 0)),
            ],
        ),
        input_output_aliases={} if first else {count + 1: 0},
        cost_estimate=pl.CostEstimate(
            flops=rows * columns * (2 * len(pairs_of(count)) + 10 * count),
            bytes_accessed=6 * rows * columns * count,
            transcendentals=2 * rows * columns * count,
        ),
        compiler_params=pltpu.CompilerParams(vmem_limit_bytes=8 << 20),
        name="gram",
    )(table, *codes, *([] if first else before))


def replica_weights(inner, count):
    vectors = [[1.0 if r == s else 0.0 for s in range(count)] for r in range(count)]

    def product(a, b):
        total = 0.0
        for r in range(count):
            for s in range(count):
                if not zero(a[r]) and not zero(b[s]):
                    total = total + a[r] * b[s] * inner[r][s]
        return total

    while len(vectors) > 1:
        merged = []
        for at in range(0, len(vectors), 2):
            a, b = vectors[at], vectors[at + 1]
            cross = product(a, b)
            a_coef = 1.0 - cross / (2.0 * (product(a, a) + 1e-06))
            b_coef = 1.0 - cross / (2.0 * (product(b, b) + 1e-06))
            merged.append([scaled(b_coef, y) if zero(x) else scaled(a_coef, x) for x, y in zip(a, b)])
        vectors = merged
    return vectors[0]


def zero(value):
    return isinstance(value, float) and value == 0.0


def scaled(coef, value):
    return 0.0 if zero(value) else coef * value


def update_kernel(count, table, gathered, units, weight, moment, second, *outs):
    new_weight, new_moment, new_second, combined, coefs = outs

    @pl.when(pl.program_id(0) == 0)
    def _():
        total = jnp.sum(gathered[...], axis=0, keepdims=True) * 0.125
        lane = lax.broadcasted_iota(jnp.int32, total.shape, 1)

        def entry(r, s):
            at = min(r, s) * count + max(r, s)
            return jnp.sum(jnp.where(lane == at, total, 0.0), axis=1, keepdims=True)

        entries = {(r, s): entry(r, s) for r, s in pairs_of(count)}
        inner = [[entries[min(r, s), max(r, s)] for s in range(count)] for r in range(count)]
        weights = replica_weights(inner, count)
        for step in range(count):
            value = jnp.zeros((1, 1), jnp.float32)
            for replica in range(count):
                value = jnp.where(table[step] == replica, weights[replica], value)
            coefs[step : step + 1, :] = jnp.broadcast_to(value, (1, LANES))

    columns = combined.shape[1]
    lanes = pl.ds(pl.multiple_of(pl.program_id(0) * columns, LANES), columns)
    total = units[0, :, lanes] * coefs[0:1, 0:1]
    for step in range(1, count):
        total = total + units[step, :, lanes] * coefs[step : step + 1, 0:1]
    combined[...] = total
    first = 0.9 * moment[...] + 0.1 * total
    square = 0.95 * second[...] + 0.05 * total * total
    new_moment[...] = first
    new_second[...] = square
    root = jnp.sqrt(square * (1.0 / bias_second)) + 1e-08
    update = first * (1.0 / bias_first) / root + 0.1 * weight[...]
    new_weight[...] = weight[...] - 0.0003 * update


def update_rows(gathered, units, weight, moment, second, table, columns):
    count, rows, width = units.shape
    block = pl.BlockSpec((rows, columns), lambda i, table: (0, i))
    return pl.pallas_call(
        lambda *refs: update_kernel(count, *refs),
        out_shape=[jax.ShapeDtypeStruct((rows, width), jnp.float32)] * 4,
        grid_spec=pltpu.PrefetchScalarGridSpec(
            num_scalar_prefetch=1,
            grid=(width // columns,),
            in_specs=[
                pl.BlockSpec(gathered.shape, lambda i, table: (0, 0)),
                pl.BlockSpec(memory_space=pltpu.VMEM),
                block,
                block,
                block,
            ],
            out_specs=[block] * 4,
            scratch_shapes=[pltpu.VMEM((max(count, 8), LANES), jnp.float32)],
        ),
        compiler_params=pltpu.CompilerParams(vmem_limit_bytes=16 << 20),
        name="update",
    )(table, gathered, units, weight, moment, second)


def per_device(acts, cotangent, weight, moment, second):
    replicas, shards = lax.axis_size("rep"), lax.axis_size("col")
    rep_rank, col_rank = lax.axis_index("rep"), lax.axis_index("col")
    devices = replicas * shards
    rows, width = weight.shape
    columns = cotangent.shape[1]
    far_first = sorted(range(replicas), key=lambda step: (step < replicas // 2, -step))
    table = [peer(rep_rank, step, replicas) for step in far_first]
    table += [peer(col_rank, step, shards) for step in range(shards)]
    table = jnp.stack(table).astype(jnp.int32)

    def sent(block, rep_step, col_step):
        route = []
        for r in range(replicas):
            for c in range(shards):
                target = peer(r, rep_step, replicas) * shards + peer(c, col_step, shards)
                route.append((r * shards + c, target))
        return lax.ppermute(block, ("rep", "col"), route)

    half = replicas // 2
    received = {}
    for col_step in range(shards):
        runs = [far_first[:half], far_first[half:]] if col_step == 0 else [far_first]
        for run in runs:
            first = far_first.index(run[0])

            def block(table, at, first=first, col_step=col_step):
                return table[first + at] * shards + table[replicas + col_step]

            codes = gradient_tiles(acts, cotangent, table, block, len(run), rows)
            for rep_step, code in zip(run, codes):
                if rep_step or col_step:
                    code = sent(code, rep_step, col_step)
                received[rep_step, col_step] = code

    state = None
    for col_step in range(shards):
        codes = [received[step, col_step] for step in far_first]
        shape = (replicas, rows, width)
        state = gram_tiles(codes, state, table, col_step, shape, devices)
    units, sums = state
    gathered = lax.all_to_all(sums, ("rep", "col"), 0, 0, tiled=True)
    return tuple(update_rows(gathered, units, weight, moment, second, table, columns))


def solution(mesh):
    return jax.shard_map(
        per_device,
        mesh=mesh,
        in_specs=(
            P("rep", None),
            P("rep", "col"),
            P(("rep", "col"), None),
            P(("rep", "col"), None),
            P(("rep", "col"), None),
        ),
        out_specs=(
            P(("rep", "col"), None),
            P(("rep", "col"), None),
            P(("rep", "col"), None),
            P(("rep", "col"), None),
        ),
        check_vma=False,
    )
```

```python
import math

import jax
import jax.numpy as jnp
from jax import lax
from jax.experimental import pallas as pl
from jax.experimental.pallas import tpu as pltpu
from jax.sharding import PartitionSpec as P

bias_first = 0.9999734386011124
bias_second = 0.99407947077966


TOP = 2.0**7.875
TINY = 1e-30
LANES, PAD, SCALE = 128, 16, 8


def peer(rank, step, count):
    if count & (count - 1) == 0:
        return rank ^ step
    return (step - rank) % count


def encode(block, largest):
    unit = jnp.abs(block) * (TOP / jnp.maximum(largest, TINY))
    power = unit * unit
    power = power * power
    power = power * power
    power = power * power
    return jnp.where(block < 0, -power, power).astype(jnp.bfloat16)


def decode(code, scale):
    code = code.astype(jnp.float32)
    unit = jnp.exp2(jnp.log2(jnp.abs(code)) * (1.0 / 16.0)) * scale
    return jnp.where(code < 0, -unit, unit)


def scale_of(block):
    largest = jnp.max(jnp.abs(block), keepdims=True) * (1.0 + 2.0**-7)
    return largest.astype(jnp.bfloat16)


def packed_shape(rows, columns):
    return (rows * columns // LANES + SCALE, LANES)


def gradient_kernel(count, *refs):
    acts, cotangent, codes = refs[1 : 1 + count], refs[1 + count], refs[2 + count :]
    rows, columns = acts[0].shape[1], cotangent.shape[1]
    left = jnp.concatenate([ref[...] for ref in acts], axis=1)
    gradient = lax.dot_general(
        left, cotangent[...], (((0,), (0,)), ((), ())), preferred_element_type=jnp.float32
    )
    for at in range(count):
        block = gradient[at * rows : (at + 1) * rows]
        largest = scale_of(block)
        code = encode(block, largest.astype(jnp.float32))
        for part in range(columns // LANES):
            lanes = slice(part * LANES, (part + 1) * LANES)
            codes[at][part * rows : (part + 1) * rows, :] = code[:, lanes]
        codes[at][rows * columns // LANES :, :] = jnp.broadcast_to(largest, (SCALE, LANES))


def gradient_tiles(acts, cotangent, table, block, count, rows):
    tokens, columns = cotangent.shape
    packed = packed_shape(rows, columns)
    if rows % LANES:
        codes = []
        for at in range(count):
            left = lax.dynamic_slice_in_dim(acts, block(table, at) * rows, rows, 1)
            part = jnp.einsum("td,tc->dc", left, cotangent, preferred_element_type=jnp.float32)
            largest = scale_of(part)
            code = encode(part, largest.astype(jnp.float32))
            code = code.reshape(rows, -1, LANES).transpose(1, 0, 2).reshape(-1, LANES)
            codes.append(jnp.concatenate([code, jnp.broadcast_to(largest, (SCALE, LANES))]))
        return codes

    def block_of(at):
        return pl.BlockSpec((tokens, rows), lambda i, table: (0, block(table, at)))

    return pl.pallas_call(
        lambda *refs: gradient_kernel(count, *refs),
        out_shape=[jax.ShapeDtypeStruct(packed, jnp.bfloat16)] * count,
        grid_spec=pltpu.PrefetchScalarGridSpec(
            num_scalar_prefetch=1,
            grid=(1,),
            in_specs=[block_of(at) for at in range(count)]
            + [pl.BlockSpec((tokens, columns), lambda i, table: (0, 0))],
            out_specs=[pl.BlockSpec(packed, lambda i, table: (0, 0))] * count,
        ),
        cost_estimate=pl.CostEstimate(
            flops=2 * tokens * rows * columns * count,
            bytes_accessed=2 * tokens * (rows * count + columns) + 2 * rows * columns * count,
            transcendentals=0,
        ),
        name="gradient",
    )(table, *([acts] * count), cotangent)


def pairs_of(count):
    return [(a, b) for a in range(count) for b in range(a, count)]


def gram_kernel(count, step, first, table, *refs):
    codes = refs[:count]
    units, sums = refs[-2], refs[-1]
    rows = units.shape[1]
    columns = (codes[0].shape[0] - SCALE) * LANES // rows
    left = pl.multiple_of(table[count + step] * columns, LANES)
    pairs = pairs_of(count)
    scales = [ref[-SCALE:, :].astype(jnp.float32)[0:1] * (1.0 / TOP) for ref in codes]

    def body(at, carry):
        carry = list(carry)
        row = pl.multiple_of(at * PAD, PAD)
        for part in range(columns // LANES):
            values = [
                decode(ref[pl.ds(part * rows + row, PAD), :], scale)
                for ref, scale in zip(codes, scales)
            ]
            for replica, value in enumerate(values):
                units[replica, pl.ds(row, PAD), pl.ds(left + part * LANES, LANES)] = value
            for index, (a, b) in enumerate(pairs):
                carry[index] = carry[index] + values[a] * values[b]
        return tuple(carry)

    zero = jnp.zeros((PAD, LANES), jnp.float32)
    carry = lax.fori_loop(0, rows // PAD, body, (zero,) * len(pairs))
    lane = lax.broadcasted_iota(jnp.int32, (8, sums.shape[1]), 1)
    total = jnp.zeros((8, sums.shape[1]), jnp.float32) if first else refs[count + 1][...]
    for value, (a, b) in zip(carry, pairs):
        value = jnp.sum(value, keepdims=True)
        here = lane == table[a] * count + table[b]
        here = here | (lane == table[b] * count + table[a])
        total = total + jnp.where(here, value, 0.0)
    sums[...] = jnp.concatenate([total] * (sums.shape[0] // 8), axis=0)


def gram_tiles(codes, before, table, step, shape, devices):
    count, rows, width = shape
    packed = codes[0].shape
    columns = (packed[0] - SCALE) * LANES // rows
    wide = -(-count * count // LANES) * LANES
    first = before is None
    extra = [] if first else [pl.BlockSpec(memory_space=pltpu.VMEM), pl.BlockSpec((8, wide), lambda i, table: (0, 0))]
    return pl.pallas_call(
        lambda *refs: gram_kernel(count, step, first, *refs),
        out_shape=[
            jax.ShapeDtypeStruct(shape, jnp.float32),
            jax.ShapeDtypeStruct((devices * 8, wide), jnp.float32),
        ],
        grid_spec=pltpu.PrefetchScalarGridSpec(
            num_scalar_prefetch=1,
            grid=(1,),
            in_specs=[pl.BlockSpec(packed, lambda i, table: (0, 0))] * count + extra,
            out_specs=[
                pl.BlockSpec(memory_space=pltpu.VMEM),
                pl.BlockSpec((devices * 8, wide), lambda i, table: (0, 0)),
            ],
        ),
        input_output_aliases={} if first else {count + 1: 0},
        cost_estimate=pl.CostEstimate(
            flops=rows * columns * (2 * len(pairs_of(count)) + 10 * count),
            bytes_accessed=6 * rows * columns * count,
            transcendentals=2 * rows * columns * count,
        ),
        compiler_params=pltpu.CompilerParams(vmem_limit_bytes=8 << 20),
        name="gram",
    )(table, *codes, *([] if first else before))


def replica_weights(inner, count):
    vectors = [[1.0 if r == s else 0.0 for s in range(count)] for r in range(count)]

    def product(a, b):
        total = 0.0
        for r in range(count):
            for s in range(count):
                if not zero(a[r]) and not zero(b[s]):
                    total = total + a[r] * b[s] * inner[r][s]
        return total

    while len(vectors) > 1:
        merged = []
        for at in range(0, len(vectors), 2):
            a, b = vectors[at], vectors[at + 1]
            cross = product(a, b)
            a_coef = 1.0 - cross / (2.0 * (product(a, a) + 1e-06))
            b_coef = 1.0 - cross / (2.0 * (product(b, b) + 1e-06))
            merged.append([scaled(b_coef, y) if zero(x) else scaled(a_coef, x) for x, y in zip(a, b)])
        vectors = merged
    return vectors[0]


def zero(value):
    return isinstance(value, float) and value == 0.0


def scaled(coef, value):
    return 0.0 if zero(value) else coef * value


def update_kernel(count, table, gathered, units, weight, moment, second, *outs):
    new_weight, new_moment, new_second, combined, coefs = outs

    @pl.when(pl.program_id(0) == 0)
    def _():
        total = jnp.sum(gathered[...], axis=0, keepdims=True) * 0.125
        lane = lax.broadcasted_iota(jnp.int32, total.shape, 1)

        def entry(r, s):
            at = min(r, s) * count + max(r, s)
            return jnp.sum(jnp.where(lane == at, total, 0.0), axis=1, keepdims=True)

        entries = {(r, s): entry(r, s) for r, s in pairs_of(count)}
        inner = [[entries[min(r, s), max(r, s)] for s in range(count)] for r in range(count)]
        weights = replica_weights(inner, count)
        for step in range(count):
            value = jnp.zeros((1, 1), jnp.float32)
            for replica in range(count):
                value = jnp.where(table[step] == replica, weights[replica], value)
            coefs[step : step + 1, :] = jnp.broadcast_to(value, (1, LANES))

    columns = combined.shape[1]
    lanes = pl.ds(pl.multiple_of(pl.program_id(0) * columns, LANES), columns)
    total = units[0, :, lanes] * coefs[0:1, 0:1]
    for step in range(1, count):
        total = total + units[step, :, lanes] * coefs[step : step + 1, 0:1]
    combined[...] = total
    first = 0.9 * moment[:, lanes] + 0.1 * total
    square = 0.95 * second[:, lanes] + 0.05 * total * total
    new_moment[...] = first
    new_second[...] = square
    root = square * lax.rsqrt(square) + 1e-08 * math.sqrt(bias_second)
    update = first * (0.0003 * math.sqrt(bias_second) / bias_first) * pl.reciprocal(root)
    new_weight[...] = weight[:, lanes] * (1.0 - 0.0003 * 0.1) - update


def update_rows(gathered, units, weight, moment, second, table, columns):
    count, rows, width = units.shape
    block = pl.BlockSpec((rows, columns), lambda i, table: (0, i))
    return pl.pallas_call(
        lambda *refs: update_kernel(count, *refs),
        out_shape=[jax.ShapeDtypeStruct((rows, width), jnp.float32)] * 4,
        grid_spec=pltpu.PrefetchScalarGridSpec(
            num_scalar_prefetch=1,
            grid=(width // columns,),
            in_specs=[
                pl.BlockSpec(gathered.shape, lambda i, table: (0, 0)),
                pl.BlockSpec(memory_space=pltpu.VMEM),
                pl.BlockSpec(memory_space=pltpu.VMEM),
                pl.BlockSpec(memory_space=pltpu.VMEM),
                pl.BlockSpec(memory_space=pltpu.VMEM),
            ],
            out_specs=[block] * 4,
            scratch_shapes=[pltpu.VMEM((max(count, 8), LANES), jnp.float32)],
        ),
        compiler_params=pltpu.CompilerParams(vmem_limit_bytes=16 << 20),
        name="update",
    )(table, gathered, units, weight, moment, second)


def per_device(acts, cotangent, weight, moment, second):
    replicas, shards = lax.axis_size("rep"), lax.axis_size("col")
    rep_rank, col_rank = lax.axis_index("rep"), lax.axis_index("col")
    devices = replicas * shards
    rows, width = weight.shape
    columns = cotangent.shape[1]
    far_first = sorted(range(replicas), key=lambda step: (step < replicas // 2, -step))
    table = [peer(rep_rank, step, replicas) for step in far_first]
    table += [peer(col_rank, step, shards) for step in range(shards)]
    table = jnp.stack(table).astype(jnp.int32)

    def sent(block, rep_step, col_step):
        route = []
        for r in range(replicas):
            for c in range(shards):
                target = peer(r, rep_step, replicas) * shards + peer(c, col_step, shards)
                route.append((r * shards + c, target))
        return lax.ppermute(block, ("rep", "col"), route)

    half = replicas // 2
    steps = [[(at, step) for at in range(replicas)] for step in range(shards)]
    runs = [steps[0][:half], steps[0][half:], steps[1]]
    runs += [sum(steps[at : at + 2], []) for at in range(2, shards, 2)]
    received = {}
    for run in runs:

        def block(table, index, run=run):
            at, col_step = run[index]
            return table[at] * shards + table[replicas + col_step]

        codes = gradient_tiles(acts, cotangent, table, block, len(run), rows)
        for (at, col_step), code in zip(run, codes):
            if far_first[at] or col_step:
                code = sent(code, far_first[at], col_step)
            received[at, col_step] = code

    state = None
    for col_step in range(shards):
        codes = [received[at, col_step] for at in range(replicas)]
        shape = (replicas, rows, width)
        state = gram_tiles(codes, state, table, col_step, shape, devices)
    units, sums = state
    gathered = lax.all_to_all(sums, ("rep", "col"), 0, 0, tiled=True)
    return tuple(update_rows(gathered, units, weight, moment, second, table, columns))


def solution(mesh):
    return jax.shard_map(
        per_device,
        mesh=mesh,
        in_specs=(
            P("rep", None),
            P("rep", "col"),
            P(("rep", "col"), None),
            P(("rep", "col"), None),
            P(("rep", "col"), None),
        ),
        out_specs=(
            P(("rep", "col"), None),
            P(("rep", "col"), None),
            P(("rep", "col"), None),
            P(("rep", "col"), None),
        ),
        check_vma=False,
    )
```

```python
import math

import jax
import jax.numpy as jnp
from jax import lax
from jax.experimental import pallas as pl
from jax.experimental.pallas import tpu as pltpu
from jax.sharding import PartitionSpec as P

bias_first = 0.9999734386011124
bias_second = 0.99407947077966


TOP = 2.0**7.875
TINY = 1e-30
LANES, PAD, SCALE = 128, 16, 8


def peer(rank, step, count):
    if count & (count - 1) == 0:
        return rank ^ step
    return (step - rank) % count


def encode(block, largest):
    unit = jnp.abs(block) * (TOP / jnp.maximum(largest, TINY))
    power = unit * unit
    power = power * power
    power = power * power
    power = power * power
    return jnp.where(block < 0, -power, power).astype(jnp.bfloat16)


def decode(code, scale):
    code = code.astype(jnp.float32)
    unit = jnp.exp2(jnp.log2(jnp.abs(code)) * (1.0 / 16.0)) * scale
    return jnp.where(code < 0, -unit, unit)


def slots(count):
    return sorted(range(count), key=lambda step: (step < count // 2, -step))


def replica_at(at, count):
    return peer(lax.axis_index("rep"), slots(count)[at], count)


def shard_at(step, count):
    return peer(lax.axis_index("col"), step, count)


def scale_of(block):
    largest = jnp.max(jnp.abs(block), keepdims=True) * (1.0 + 2.0**-7)
    return largest.astype(jnp.bfloat16)


def packed_shape(rows, columns):
    return (rows * columns // LANES + SCALE, LANES)


def gradient_kernel(count, *refs):
    acts, cotangent, codes = refs[:count], refs[count], refs[count + 1 :]
    rows, columns = acts[0].shape[1], cotangent.shape[1]
    left = jnp.concatenate([ref[...] for ref in acts], axis=1)
    gradient = lax.dot_general(
        left, cotangent[...], (((0,), (0,)), ((), ())), preferred_element_type=jnp.float32
    )
    for at in range(count):
        block = gradient[at * rows : (at + 1) * rows]
        largest = scale_of(block)
        code = encode(block, largest.astype(jnp.float32))
        for part in range(columns // LANES):
            lanes = slice(part * LANES, (part + 1) * LANES)
            codes[at][part * rows : (part + 1) * rows, :] = code[:, lanes]
        codes[at][rows * columns // LANES :, :] = jnp.broadcast_to(largest, (SCALE, LANES))


def gradient_tiles(acts, cotangent, block, count, rows):
    tokens, columns = cotangent.shape
    packed = packed_shape(rows, columns)
    if rows % LANES:
        codes = []
        for at in range(count):
            left = lax.dynamic_slice_in_dim(acts, block(at) * rows, rows, 1)
            part = jnp.einsum("td,tc->dc", left, cotangent, preferred_element_type=jnp.float32)
            largest = scale_of(part)
            code = encode(part, largest.astype(jnp.float32))
            code = code.reshape(rows, -1, LANES).transpose(1, 0, 2).reshape(-1, LANES)
            codes.append(jnp.concatenate([code, jnp.broadcast_to(largest, (SCALE, LANES))]))
        return codes

    def block_of(at):
        return pl.BlockSpec((tokens, rows), lambda i: (0, block(at)))

    return pl.pallas_call(
        lambda *refs: gradient_kernel(count, *refs),
        out_shape=[jax.ShapeDtypeStruct(packed, jnp.bfloat16)] * count,
        grid=(1,),
        in_specs=[block_of(at) for at in range(count)]
        + [pl.BlockSpec((tokens, columns), lambda i: (0, 0))],
        out_specs=[pl.BlockSpec(packed, lambda i: (0, 0))] * count,
        cost_estimate=pl.CostEstimate(
            flops=2 * tokens * rows * columns * count,
            bytes_accessed=2 * tokens * (rows * count + columns) + 2 * rows * columns * count,
            transcendentals=0,
        ),
        name="gradient",
    )(*([acts] * count), cotangent)


def pairs_of(count):
    return [(a, b) for a in range(count) for b in range(a, count)]


def gram_kernel(count, step, first, shards, *refs):
    codes = refs[:count]
    units, sums = refs[-2], refs[-1]
    rows = units.shape[1]
    columns = (codes[0].shape[0] - SCALE) * LANES // rows
    left = pl.multiple_of(shard_at(step, shards) * columns, LANES)
    pairs = pairs_of(count)
    scales = [ref[-SCALE:, :].astype(jnp.float32)[0:1] * (1.0 / TOP) for ref in codes]

    def body(at, carry):
        carry = list(carry)
        row = pl.multiple_of(at * PAD, PAD)
        for part in range(columns // LANES):
            values = [
                decode(ref[pl.ds(part * rows + row, PAD), :], scale)
                for ref, scale in zip(codes, scales)
            ]
            for replica, value in enumerate(values):
                units[replica, pl.ds(row, PAD), pl.ds(left + part * LANES, LANES)] = value
            for index, (a, b) in enumerate(pairs):
                carry[index] = carry[index] + values[a] * values[b]
        return tuple(carry)

    zero = jnp.zeros((PAD, LANES), jnp.float32)
    carry = lax.fori_loop(0, rows // PAD, body, (zero,) * len(pairs))
    lane = lax.broadcasted_iota(jnp.int32, (8, sums.shape[1]), 1)
    total = jnp.zeros((8, sums.shape[1]), jnp.float32) if first else refs[count + 1][...]
    for value, (a, b) in zip(carry, pairs):
        value = jnp.sum(value, keepdims=True)
        a, b = replica_at(a, count), replica_at(b, count)
        here = lane == a * count + b
        here = here | (lane == b * count + a)
        total = total + jnp.where(here, value, 0.0)
    sums[...] = jnp.concatenate([total] * (sums.shape[0] // 8), axis=0)


def gram_tiles(codes, before, step, shape, shards):
    count, rows, width = shape
    packed = codes[0].shape
    columns = (packed[0] - SCALE) * LANES // rows
    devices = count * shards
    wide = -(-count * count // LANES) * LANES
    first = before is None
    extra = [] if first else [pl.BlockSpec(memory_space=pltpu.VMEM), pl.BlockSpec((8, wide), lambda i: (0, 0))]
    return pl.pallas_call(
        lambda *refs: gram_kernel(count, step, first, shards, *refs),
        out_shape=[
            jax.ShapeDtypeStruct(shape, jnp.float32),
            jax.ShapeDtypeStruct((devices * 8, wide), jnp.float32),
        ],
        grid=(1,),
        in_specs=[pl.BlockSpec(packed, lambda i: (0, 0))] * count + extra,
        out_specs=[
            pl.BlockSpec(memory_space=pltpu.VMEM),
            pl.BlockSpec((devices * 8, wide), lambda i: (0, 0)),
        ],
        input_output_aliases={} if first else {count: 0},
        cost_estimate=pl.CostEstimate(
            flops=rows * columns * (2 * len(pairs_of(count)) + 10 * count),
            bytes_accessed=6 * rows * columns * count,
            transcendentals=2 * rows * columns * count,
        ),
        compiler_params=pltpu.CompilerParams(vmem_limit_bytes=8 << 20),
        name="gram",
    )(*codes, *([] if first else before))


def replica_weights(inner, count):
    vectors = [[1.0 if r == s else 0.0 for s in range(count)] for r in range(count)]

    def product(a, b):
        total = 0.0
        for r in range(count):
            for s in range(count):
                if not zero(a[r]) and not zero(b[s]):
                    total = total + a[r] * b[s] * inner[r][s]
        return total

    while len(vectors) > 1:
        merged = []
        for at in range(0, len(vectors), 2):
            a, b = vectors[at], vectors[at + 1]
            cross = product(a, b)
            a_coef = 1.0 - cross / (2.0 * (product(a, a) + 1e-06))
            b_coef = 1.0 - cross / (2.0 * (product(b, b) + 1e-06))
            merged.append([scaled(b_coef, y) if zero(x) else scaled(a_coef, x) for x, y in zip(a, b)])
        vectors = merged
    return vectors[0]


def zero(value):
    return isinstance(value, float) and value == 0.0


def scaled(coef, value):
    return 0.0 if zero(value) else coef * value


def update_kernel(count, gathered, units, weight, moment, second, *outs):
    new_weight, new_moment, new_second, combined, coefs = outs

    @pl.when(pl.program_id(0) == 0)
    def _():
        total = jnp.sum(gathered[...], axis=0, keepdims=True) * 0.125
        lane = lax.broadcasted_iota(jnp.int32, total.shape, 1)

        def entry(r, s):
            at = min(r, s) * count + max(r, s)
            return jnp.sum(jnp.where(lane == at, total, 0.0), axis=1, keepdims=True)

        entries = {(r, s): entry(r, s) for r, s in pairs_of(count)}
        inner = [[entries[min(r, s), max(r, s)] for s in range(count)] for r in range(count)]
        weights = replica_weights(inner, count)
        for step in range(count):
            value = jnp.zeros((1, 1), jnp.float32)
            for replica in range(count):
                value = jnp.where(replica_at(step, count) == replica, weights[replica], value)
            coefs[step : step + 1, :] = jnp.broadcast_to(value, (1, LANES))

    rows, width = combined.shape
    top = pl.program_id(0) * rows
    mixing = [jnp.broadcast_to(coefs[step : step + 1, 0:1], (8, 2 * LANES)) for step in range(count)]
    for at in range(0, rows, 8):
        row, there = pl.ds(pl.multiple_of(top + at, 8), 8), slice(at, at + 8)
        for part in range(0, width, 2 * LANES):
            here = slice(part, part + 2 * LANES)
            total = units[0, row, here] * mixing[0]
            for step in range(1, count):
                total = total + units[step, row, here] * mixing[step]
            first = 0.9 * moment[row, here] + 0.1 * total
            square = 0.95 * second[row, here] + 0.05 * total * total
            root = square * lax.rsqrt(square) + 1e-08 * math.sqrt(bias_second)
            change = first * (0.0003 * math.sqrt(bias_second) / bias_first) * pl.reciprocal(root)
            combined[there, here] = total
            new_moment[there, here] = first
            new_second[there, here] = square
            new_weight[there, here] = weight[row, here] * (1.0 - 0.0003 * 0.1) - change


def update_rows(gathered, units, weight, moment, second):
    count, rows, width = units.shape
    block = pl.BlockSpec((PAD, width), lambda i: (i, 0))
    return pl.pallas_call(
        lambda *refs: update_kernel(count, *refs),
        out_shape=[jax.ShapeDtypeStruct((rows, width), jnp.float32)] * 4,
        grid=(rows // PAD,),
        in_specs=[pl.BlockSpec(gathered.shape, lambda i: (0, 0))]
        + [pl.BlockSpec(memory_space=pltpu.VMEM)] * 4,
        out_specs=[block] * 4,
        scratch_shapes=[pltpu.VMEM((max(count, 8), LANES), jnp.float32)],
        compiler_params=pltpu.CompilerParams(vmem_limit_bytes=16 << 20),
        name="update",
    )(gathered, units, weight, moment, second)


def per_device(acts, cotangent, weight, moment, second):
    replicas, shards = lax.axis_size("rep"), lax.axis_size("col")
    rows, width = weight.shape
    far_first = slots(replicas)

    def sent(block, rep_step, col_step):
        route = []
        for r in range(replicas):
            for c in range(shards):
                target = peer(r, rep_step, replicas) * shards + peer(c, col_step, shards)
                route.append((r * shards + c, target))
        return lax.ppermute(block, ("rep", "col"), route)

    half = replicas // 2
    steps = [[(at, step) for at in range(replicas)] for step in range(shards)]
    runs = [steps[0][:half], steps[0][half:], steps[1]]
    runs += [sum(steps[at : at + 2], []) for at in range(2, shards, 2)]
    received = {}
    for run in runs:

        def block(index, run=run):
            at, col_step = run[index]
            return replica_at(at, replicas) * shards + shard_at(col_step, shards)

        codes = gradient_tiles(acts, cotangent, block, len(run), rows)
        for (at, col_step), code in zip(run, codes):
            if far_first[at] or col_step:
                code = sent(code, far_first[at], col_step)
            received[at, col_step] = code

    state = None
    for col_step in range(shards):
        codes = [received[at, col_step] for at in range(replicas)]
        shape = (replicas, rows, width)
        state = gram_tiles(codes, state, col_step, shape, shards)
    units, sums = state
    gathered = lax.all_to_all(sums, ("rep", "col"), 0, 0, tiled=True)
    return tuple(update_rows(gathered, units, weight, moment, second))


def solution(mesh):
    return jax.shard_map(
        per_device,
        mesh=mesh,
        in_specs=(
            P("rep", None),
            P("rep", "col"),
            P(("rep", "col"), None),
            P(("rep", "col"), None),
            P(("rep", "col"), None),
        ),
        out_specs=(
            P(("rep", "col"), None),
            P(("rep", "col"), None),
            P(("rep", "col"), None),
            P(("rep", "col"), None),
        ),
        check_vma=False,
    )
```

```python
import math

import jax
import jax.numpy as jnp
from jax import lax
from jax.experimental import pallas as pl
from jax.experimental.pallas import tpu as pltpu
from jax.sharding import PartitionSpec as P

bias_first = 0.9999734386011124
bias_second = 0.99407947077966


TOP = 2.0**7.875
TINY = 1e-30
LANES, PAD, SCALE = 128, 16, 8
SPLIT = 4


def peer(rank, step, count):
    if count & (count - 1) == 0:
        return rank ^ step
    return (step - rank) % count


def encode(block, largest):
    unit = jnp.abs(block) * (TOP / jnp.maximum(largest, TINY))
    power = unit * unit
    power = power * power
    power = power * power
    power = power * power
    return jnp.where(block < 0, -power, power).astype(jnp.bfloat16)


def decode(code, scale):
    code = code.astype(jnp.float32)
    unit = jnp.exp2(jnp.log2(jnp.abs(code)) * (1.0 / 16.0)) * scale
    return jnp.where(code < 0, -unit, unit)


def slots(count):
    return sorted(range(count), key=lambda step: (step < count // 2, -step))


def replica_at(at, count):
    return peer(lax.axis_index("rep"), slots(count)[at], count)


def shard_at(step, count):
    return peer(lax.axis_index("col"), step, count)


def scale_of(block):
    largest = jnp.max(jnp.abs(block), keepdims=True) * (1.0 + 2.0**-7)
    return largest.astype(jnp.bfloat16)


def packed_shape(rows, columns):
    return (rows * columns // LANES + SCALE, LANES)


def gradient_kernel(count, block, rows, acts, cotangent, *refs):
    codes, (lefts, rights, arrived) = refs[:count], refs[count:]
    tokens, columns = cotangent.shape
    part = tokens // SPLIT

    def copies(chunk):
        window = pl.ds(chunk * part, part)
        moves = [(cotangent.at[window, :], rights.at[window, :])]
        for at in range(count):
            source = acts.at[window, pl.ds(pl.multiple_of(block(at) * rows, LANES), rows)]
            moves.append((source, lefts.at[window, at * rows : (at + 1) * rows]))
        return [
            pltpu.make_async_copy(source, target, arrived.at[chunk, at])
            for at, (source, target) in enumerate(moves)
        ]

    pending = [copies(chunk) for chunk in range(SPLIT)]
    for moves in pending:
        for move in moves:
            move.start()
    gradient = None
    for chunk, moves in enumerate(pending):
        for move in moves:
            move.wait()
        window = slice(chunk * part, (chunk + 1) * part)
        product = lax.dot_general(
            lefts[window, :],
            rights[window, :],
            (((0,), (0,)), ((), ())),
            preferred_element_type=jnp.float32,
        )
        gradient = product if gradient is None else gradient + product
    for at in range(count):
        tile = gradient[at * rows : (at + 1) * rows]
        largest = scale_of(tile)
        code = encode(tile, largest.astype(jnp.float32))
        for piece in range(columns // LANES):
            lanes = slice(piece * LANES, (piece + 1) * LANES)
            codes[at][piece * rows : (piece + 1) * rows, :] = code[:, lanes]
        codes[at][rows * columns // LANES :, :] = jnp.broadcast_to(largest, (SCALE, LANES))


def gradient_tiles(acts, cotangent, block, count, rows):
    tokens, columns = cotangent.shape
    packed = packed_shape(rows, columns)
    if rows % LANES or tokens % (SPLIT * PAD):
        codes = []
        for at in range(count):
            left = lax.dynamic_slice_in_dim(acts, block(at) * rows, rows, 1)
            part = jnp.einsum("td,tc->dc", left, cotangent, preferred_element_type=jnp.float32)
            largest = scale_of(part)
            code = encode(part, lax.reduce_precision(largest.astype(jnp.float32), 8, 7))
            code = code.reshape(rows, -1, LANES).transpose(1, 0, 2).reshape(-1, LANES)
            codes.append(jnp.concatenate([code, jnp.broadcast_to(largest, (SCALE, LANES))]))
        return codes

    return pl.pallas_call(
        lambda *refs: gradient_kernel(count, block, rows, *refs),
        out_shape=[jax.ShapeDtypeStruct(packed, jnp.bfloat16)] * count,
        grid=(1,),
        in_specs=[pl.BlockSpec(memory_space=pl.ANY)] * 2,
        out_specs=[pl.BlockSpec(packed, lambda i: (0, 0))] * count,
        scratch_shapes=[
            pltpu.VMEM((tokens, count * rows), jnp.bfloat16),
            pltpu.VMEM((tokens, columns), jnp.bfloat16),
            pltpu.SemaphoreType.DMA((SPLIT, count + 1)),
        ],
        cost_estimate=pl.CostEstimate(
            flops=2 * tokens * rows * columns * count,
            bytes_accessed=2 * tokens * (rows * count + columns) + 2 * rows * columns * count,
            transcendentals=0,
        ),
        name="gradient",
    )(acts, cotangent)


def pairs_of(count):
    return [(a, b) for a in range(count) for b in range(a, count)]


def gram_kernel(count, step, first, shards, *refs):
    codes = refs[:count]
    units, sums = refs[-2], refs[-1]
    rows = units.shape[1]
    columns = (codes[0].shape[0] - SCALE) * LANES // rows
    left = pl.multiple_of(shard_at(step, shards) * columns, LANES)
    pairs = pairs_of(count)
    scales = [ref[-SCALE:, :].astype(jnp.float32)[0:1] * (1.0 / TOP) for ref in codes]

    def body(at, carry):
        carry = list(carry)
        row = pl.multiple_of(at * PAD, PAD)
        for part in range(columns // LANES):
            values = [
                decode(ref[pl.ds(part * rows + row, PAD), :], scale)
                for ref, scale in zip(codes, scales)
            ]
            for replica, value in enumerate(values):
                units[replica, pl.ds(row, PAD), pl.ds(left + part * LANES, LANES)] = value
            for index, (a, b) in enumerate(pairs):
                carry[index] = carry[index] + values[a] * values[b]
        return tuple(carry)

    zero = jnp.zeros((PAD, LANES), jnp.float32)
    carry = lax.fori_loop(0, rows // PAD, body, (zero,) * len(pairs))
    lane = lax.broadcasted_iota(jnp.int32, (8, sums.shape[1]), 1)
    total = jnp.zeros((8, sums.shape[1]), jnp.float32) if first else refs[count + 1][...]
    for value, (a, b) in zip(carry, pairs):
        value = jnp.sum(value, keepdims=True)
        a, b = replica_at(a, count), replica_at(b, count)
        here = lane == a * count + b
        here = here | (lane == b * count + a)
        total = total + jnp.where(here, value, 0.0)
    sums[...] = jnp.concatenate([total] * (sums.shape[0] // 8), axis=0)


def gram_tiles(codes, before, step, shape, shards):
    count, rows, width = shape
    packed = codes[0].shape
    columns = (packed[0] - SCALE) * LANES // rows
    devices = count * shards
    wide = -(-count * count // LANES) * LANES
    first = before is None
    extra = [] if first else [pl.BlockSpec(memory_space=pltpu.VMEM), pl.BlockSpec((8, wide), lambda i: (0, 0))]
    return pl.pallas_call(
        lambda *refs: gram_kernel(count, step, first, shards, *refs),
        out_shape=[
            jax.ShapeDtypeStruct(shape, jnp.float32),
            jax.ShapeDtypeStruct((devices * 8, wide), jnp.float32),
        ],
        grid=(1,),
        in_specs=[pl.BlockSpec(packed, lambda i: (0, 0))] * count + extra,
        out_specs=[
            pl.BlockSpec(memory_space=pltpu.VMEM),
            pl.BlockSpec((devices * 8, wide), lambda i: (0, 0)),
        ],
        input_output_aliases={} if first else {count: 0},
        cost_estimate=pl.CostEstimate(
            flops=rows * columns * (2 * len(pairs_of(count)) + 10 * count),
            bytes_accessed=6 * rows * columns * count,
            transcendentals=2 * rows * columns * count,
        ),
        compiler_params=pltpu.CompilerParams(vmem_limit_bytes=8 << 20),
        name="gram",
    )(*codes, *([] if first else before))


def replica_weights(inner, count):
    vectors = [[1.0 if r == s else 0.0 for s in range(count)] for r in range(count)]

    def product(a, b):
        total = 0.0
        for r in range(count):
            for s in range(count):
                if not zero(a[r]) and not zero(b[s]):
                    total = total + a[r] * b[s] * inner[r][s]
        return total

    while len(vectors) > 1:
        merged = []
        for at in range(0, len(vectors), 2):
            a, b = vectors[at], vectors[at + 1]
            cross = product(a, b)
            a_coef = 1.0 - cross / (2.0 * (product(a, a) + 1e-06))
            b_coef = 1.0 - cross / (2.0 * (product(b, b) + 1e-06))
            merged.append([scaled(b_coef, y) if zero(x) else scaled(a_coef, x) for x, y in zip(a, b)])
        vectors = merged
    return vectors[0]


def zero(value):
    return isinstance(value, float) and value == 0.0


def scaled(coef, value):
    return 0.0 if zero(value) else coef * value


def update_kernel(count, gathered, units, weight, moment, second, *outs):
    new_weight, new_moment, new_second, combined, coefs = outs

    @pl.when(pl.program_id(0) == 0)
    def _():
        total = jnp.sum(gathered[...], axis=0, keepdims=True) * 0.125
        lane = lax.broadcasted_iota(jnp.int32, total.shape, 1)

        def entry(r, s):
            at = min(r, s) * count + max(r, s)
            return jnp.sum(jnp.where(lane == at, total, 0.0), axis=1, keepdims=True)

        entries = {(r, s): entry(r, s) for r, s in pairs_of(count)}
        inner = [[entries[min(r, s), max(r, s)] for s in range(count)] for r in range(count)]
        weights = replica_weights(inner, count)
        for step in range(count):
            value = jnp.zeros((1, 1), jnp.float32)
            for replica in range(count):
                value = jnp.where(replica_at(step, count) == replica, weights[replica], value)
            coefs[step : step + 1, :] = jnp.broadcast_to(value, (1, LANES))

    rows, width = combined.shape
    top = pl.program_id(0) * rows
    mixing = [jnp.broadcast_to(coefs[step : step + 1, 0:1], (8, 2 * LANES)) for step in range(count)]
    for at in range(0, rows, 8):
        row, there = pl.ds(pl.multiple_of(top + at, 8), 8), slice(at, at + 8)
        for part in range(0, width, 2 * LANES):
            here = slice(part, part + 2 * LANES)
            total = units[0, row, here] * mixing[0]
            for step in range(1, count):
                total = total + units[step, row, here] * mixing[step]
            first = 0.9 * moment[row, here] + 0.1 * total
            square = 0.95 * second[row, here] + 0.05 * total * total
            root = square * lax.rsqrt(square) + 1e-08 * math.sqrt(bias_second)
            change = first * (0.0003 * math.sqrt(bias_second) / bias_first) * pl.reciprocal(root)
            combined[there, here] = total
            new_moment[there, here] = first
            new_second[there, here] = square
            new_weight[there, here] = weight[row, here] * (1.0 - 0.0003 * 0.1) - change


def update_rows(gathered, units, weight, moment, second):
    count, rows, width = units.shape
    block = pl.BlockSpec((PAD, width), lambda i: (i, 0))
    return pl.pallas_call(
        lambda *refs: update_kernel(count, *refs),
        out_shape=[jax.ShapeDtypeStruct((rows, width), jnp.float32)] * 4,
        grid=(rows // PAD,),
        in_specs=[pl.BlockSpec(gathered.shape, lambda i: (0, 0))]
        + [pl.BlockSpec(memory_space=pltpu.VMEM)] * 4,
        out_specs=[block] * 4,
        scratch_shapes=[pltpu.VMEM((max(count, 8), LANES), jnp.float32)],
        compiler_params=pltpu.CompilerParams(vmem_limit_bytes=16 << 20),
        name="update",
    )(gathered, units, weight, moment, second)


def per_device(acts, cotangent, weight, moment, second):
    replicas, shards = lax.axis_size("rep"), lax.axis_size("col")
    rows, width = weight.shape
    far_first = slots(replicas)

    def sent(block, rep_step, col_step):
        route = []
        for r in range(replicas):
            for c in range(shards):
                target = peer(r, rep_step, replicas) * shards + peer(c, col_step, shards)
                route.append((r * shards + c, target))
        return lax.ppermute(block, ("rep", "col"), route)

    half = replicas // 2
    steps = [[(at, step) for at in range(replicas)] for step in range(shards)]
    runs = [steps[0][:half], steps[0][half:], steps[1]]
    runs += [sum(steps[at : at + 2], []) for at in range(2, shards, 2)]
    received = {}
    for run in runs:

        def block(index, run=run):
            at, col_step = run[index]
            return replica_at(at, replicas) * shards + shard_at(col_step, shards)

        codes = gradient_tiles(acts, cotangent, block, len(run), rows)
        for (at, col_step), code in zip(run, codes):
            if far_first[at] or col_step:
                code = sent(code, far_first[at], col_step)
            received[at, col_step] = code

    state = None
    for col_step in range(shards):
        codes = [received[at, col_step] for at in range(replicas)]
        shape = (replicas, rows, width)
        state = gram_tiles(codes, state, col_step, shape, shards)
    units, sums = state
    gathered = lax.all_to_all(sums, ("rep", "col"), 0, 0, tiled=True)
    return tuple(update_rows(gathered, units, weight, moment, second))


def solution(mesh):
    return jax.shard_map(
        per_device,
        mesh=mesh,
        in_specs=(
            P("rep", None),
            P("rep", "col"),
            P(("rep", "col"), None),
            P(("rep", "col"), None),
            P(("rep", "col"), None),
        ),
        out_specs=(
            P(("rep", "col"), None),
            P(("rep", "col"), None),
            P(("rep", "col"), None),
            P(("rep", "col"), None),
        ),
        check_vma=False,
    )
```

```python
import math

import jax
import jax.numpy as jnp
from jax import lax
from jax.experimental import pallas as pl
from jax.experimental.pallas import tpu as pltpu
from jax.sharding import PartitionSpec as P

bias_first = 0.9999734386011124
bias_second = 0.99407947077966


TOP = 2.0**7.875
TINY = 1e-30
LANES, PAD, SCALE = 128, 16, 8
SPLIT = 2


def peer(rank, step, count):
    if count & (count - 1) == 0:
        return rank ^ step
    return (step - rank) % count


def encode(block, largest):
    unit = jnp.abs(block) * (TOP / jnp.maximum(largest, TINY))
    power = unit * unit
    power = power * power
    power = power * power
    power = power * power
    return jnp.where(block < 0, -power, power).astype(jnp.bfloat16)


def decode(code, scale):
    code = code.astype(jnp.float32)
    unit = jnp.exp2(jnp.log2(jnp.abs(code)) * (1.0 / 16.0)) * scale
    return jnp.where(code < 0, -unit, unit)


def slots(count):
    return sorted(range(count), key=lambda step: (step < count // 2, -step))


def replica_at(at, count):
    return peer(lax.axis_index("rep"), slots(count)[at], count)


def shard_at(step, count):
    return peer(lax.axis_index("col"), step, count)


def scale_of(block):
    largest = jnp.max(jnp.abs(block), keepdims=True) * (1.0 + 2.0**-7)
    return largest.astype(jnp.bfloat16)


def packed_shape(rows, columns):
    return (rows * columns // LANES + SCALE, LANES)


def gradient_kernel(count, block, rows, acts, cotangent, *refs):
    codes, (lefts, rights, arrived) = refs[:count], refs[count:]
    tokens, columns = cotangent.shape
    part = tokens // SPLIT

    def copies(chunk):
        window = pl.ds(chunk * part, part)
        moves = [(cotangent.at[window, :], rights.at[window, :])]
        for at in range(count):
            source = acts.at[window, pl.ds(pl.multiple_of(block(at) * rows, LANES), rows)]
            moves.append((source, lefts.at[window, at * rows : (at + 1) * rows]))
        return [
            pltpu.make_async_copy(source, target, arrived.at[chunk, at])
            for at, (source, target) in enumerate(moves)
        ]

    pending = [copies(chunk) for chunk in range(SPLIT)]
    for moves in pending:
        for move in moves:
            move.start()
    gradient = None
    for chunk, moves in enumerate(pending):
        for move in moves:
            move.wait()
        window = slice(chunk * part, (chunk + 1) * part)
        product = lax.dot_general(
            lefts[window, :],
            rights[window, :],
            (((0,), (0,)), ((), ())),
            preferred_element_type=jnp.float32,
        )
        gradient = product if gradient is None else gradient + product
    for at in range(count):
        tile = gradient[at * rows : (at + 1) * rows]
        largest = scale_of(tile)
        code = encode(tile, largest.astype(jnp.float32))
        for piece in range(columns // LANES):
            lanes = slice(piece * LANES, (piece + 1) * LANES)
            codes[at][piece * rows : (piece + 1) * rows, :] = code[:, lanes]
        codes[at][rows * columns // LANES :, :] = jnp.broadcast_to(largest, (SCALE, LANES))


def gradient_tiles(acts, cotangent, block, count, rows):
    tokens, columns = cotangent.shape
    packed = packed_shape(rows, columns)
    if rows % LANES or tokens % (SPLIT * PAD):
        codes = []
        for at in range(count):
            left = lax.dynamic_slice_in_dim(acts, block(at) * rows, rows, 1)
            part = jnp.einsum("td,tc->dc", left, cotangent, preferred_element_type=jnp.float32)
            largest = scale_of(part)
            code = encode(part, lax.reduce_precision(largest.astype(jnp.float32), 8, 7))
            code = code.reshape(rows, -1, LANES).transpose(1, 0, 2).reshape(-1, LANES)
            codes.append(jnp.concatenate([code, jnp.broadcast_to(largest, (SCALE, LANES))]))
        return codes

    return pl.pallas_call(
        lambda *refs: gradient_kernel(count, block, rows, *refs),
        out_shape=[jax.ShapeDtypeStruct(packed, jnp.bfloat16)] * count,
        grid=(1,),
        in_specs=[pl.BlockSpec(memory_space=pl.ANY)] * 2,
        out_specs=[pl.BlockSpec(packed, lambda i: (0, 0))] * count,
        scratch_shapes=[
            pltpu.VMEM((tokens, count * rows), jnp.bfloat16),
            pltpu.VMEM((tokens, columns), jnp.bfloat16),
            pltpu.SemaphoreType.DMA((SPLIT, count + 1)),
        ],
        cost_estimate=pl.CostEstimate(
            flops=2 * tokens * rows * columns * count,
            bytes_accessed=2 * tokens * (rows * count + columns) + 2 * rows * columns * count,
            transcendentals=0,
        ),
        name="gradient",
    )(acts, cotangent)


def pairs_of(count):
    return [(a, b) for a in range(count) for b in range(a, count)]


def gram_kernel(count, step, first, shards, *refs):
    codes = refs[:count]
    units, sums = refs[-2], refs[-1]
    rows = units.shape[1]
    columns = (codes[0].shape[0] - SCALE) * LANES // rows
    left = pl.multiple_of(shard_at(step, shards) * columns, LANES)
    pairs = pairs_of(count)
    scales = [ref[-SCALE:, :].astype(jnp.float32)[0:1] * (1.0 / TOP) for ref in codes]

    def body(at, carry):
        carry = list(carry)
        row = pl.multiple_of(at * PAD, PAD)
        for part in range(columns // LANES):
            values = [
                decode(ref[pl.ds(part * rows + row, PAD), :], scale)
                for ref, scale in zip(codes, scales)
            ]
            for replica, value in enumerate(values):
                units[replica, pl.ds(row, PAD), pl.ds(left + part * LANES, LANES)] = value
            for index, (a, b) in enumerate(pairs):
                carry[index] = carry[index] + values[a] * values[b]
        return tuple(carry)

    zero = jnp.zeros((PAD, LANES), jnp.float32)
    carry = lax.fori_loop(0, rows // PAD, body, (zero,) * len(pairs))
    lane = lax.broadcasted_iota(jnp.int32, (8, sums.shape[1]), 1)
    total = jnp.zeros((8, sums.shape[1]), jnp.float32) if first else refs[count + 1][...]
    for value, (a, b) in zip(carry, pairs):
        value = jnp.sum(value, keepdims=True)
        a, b = replica_at(a, count), replica_at(b, count)
        here = lane == a * count + b
        here = here | (lane == b * count + a)
        total = total + jnp.where(here, value, 0.0)
    sums[...] = jnp.concatenate([total] * (sums.shape[0] // 8), axis=0)


def gram_tiles(codes, before, step, shape, shards):
    count, rows, width = shape
    packed = codes[0].shape
    columns = (packed[0] - SCALE) * LANES // rows
    devices = count * shards
    wide = -(-count * count // LANES) * LANES
    first = before is None
    extra = [] if first else [pl.BlockSpec(memory_space=pltpu.VMEM), pl.BlockSpec((8, wide), lambda i: (0, 0))]
    return pl.pallas_call(
        lambda *refs: gram_kernel(count, step, first, shards, *refs),
        out_shape=[
            jax.ShapeDtypeStruct(shape, jnp.float32),
            jax.ShapeDtypeStruct((devices * 8, wide), jnp.float32),
        ],
        grid=(1,),
        in_specs=[pl.BlockSpec(packed, lambda i: (0, 0))] * count + extra,
        out_specs=[
            pl.BlockSpec(memory_space=pltpu.VMEM),
            pl.BlockSpec((devices * 8, wide), lambda i: (0, 0)),
        ],
        input_output_aliases={} if first else {count: 0},
        cost_estimate=pl.CostEstimate(
            flops=rows * columns * (2 * len(pairs_of(count)) + 10 * count),
            bytes_accessed=6 * rows * columns * count,
            transcendentals=2 * rows * columns * count,
        ),
        compiler_params=pltpu.CompilerParams(vmem_limit_bytes=8 << 20),
        name="gram",
    )(*codes, *([] if first else before))


def replica_weights(inner, count):
    vectors = [[1.0 if r == s else 0.0 for s in range(count)] for r in range(count)]

    def product(a, b):
        total = 0.0
        for r in range(count):
            for s in range(count):
                if not zero(a[r]) and not zero(b[s]):
                    total = total + a[r] * b[s] * inner[r][s]
        return total

    while len(vectors) > 1:
        merged = []
        for at in range(0, len(vectors), 2):
            a, b = vectors[at], vectors[at + 1]
            cross = product(a, b)
            a_coef = 1.0 - cross / (2.0 * (product(a, a) + 1e-06))
            b_coef = 1.0 - cross / (2.0 * (product(b, b) + 1e-06))
            merged.append([scaled(b_coef, y) if zero(x) else scaled(a_coef, x) for x, y in zip(a, b)])
        vectors = merged
    return vectors[0]


def zero(value):
    return isinstance(value, float) and value == 0.0


def scaled(coef, value):
    return 0.0 if zero(value) else coef * value


def update_kernel(count, gathered, units, weight, moment, second, *outs):
    new_weight, new_moment, new_second, combined, coefs = outs

    @pl.when(pl.program_id(0) == 0)
    def _():
        total = jnp.sum(gathered[...], axis=0, keepdims=True) * 0.125
        lane = lax.broadcasted_iota(jnp.int32, total.shape, 1)

        def entry(r, s):
            at = min(r, s) * count + max(r, s)
            return jnp.sum(jnp.where(lane == at, total, 0.0), axis=1, keepdims=True)

        entries = {(r, s): entry(r, s) for r, s in pairs_of(count)}
        inner = [[entries[min(r, s), max(r, s)] for s in range(count)] for r in range(count)]
        weights = replica_weights(inner, count)
        for step in range(count):
            value = jnp.zeros((1, 1), jnp.float32)
            for replica in range(count):
                value = jnp.where(replica_at(step, count) == replica, weights[replica], value)
            coefs[step : step + 1, :] = jnp.broadcast_to(value, (1, LANES))

    rows, width = combined.shape
    top = pl.program_id(0) * rows
    mixing = [jnp.broadcast_to(coefs[step : step + 1, 0:1], (8, 2 * LANES)) for step in range(count)]
    for at in range(0, rows, 8):
        row, there = pl.ds(pl.multiple_of(top + at, 8), 8), slice(at, at + 8)
        for part in range(0, width, 2 * LANES):
            here = slice(part, part + 2 * LANES)
            total = units[0, row, here] * mixing[0]
            for step in range(1, count):
                total = total + units[step, row, here] * mixing[step]
            first = 0.9 * moment[row, here] + 0.1 * total
            square = 0.95 * second[row, here] + 0.05 * total * total
            root = square * lax.rsqrt(square) + 1e-08 * math.sqrt(bias_second)
            change = first * (0.0003 * math.sqrt(bias_second) / bias_first) * pl.reciprocal(root)
            combined[there, here] = total
            new_moment[there, here] = first
            new_second[there, here] = square
            new_weight[there, here] = weight[row, here] * (1.0 - 0.0003 * 0.1) - change


def update_rows(gathered, units, weight, moment, second):
    count, rows, width = units.shape
    block = pl.BlockSpec((PAD, width), lambda i: (i, 0))
    return pl.pallas_call(
        lambda *refs: update_kernel(count, *refs),
        out_shape=[jax.ShapeDtypeStruct((rows, width), jnp.float32)] * 4,
        grid=(rows // PAD,),
        in_specs=[pl.BlockSpec(gathered.shape, lambda i: (0, 0))]
        + [pl.BlockSpec(memory_space=pltpu.VMEM)] * 4,
        out_specs=[block] * 4,
        scratch_shapes=[pltpu.VMEM((max(count, 8), LANES), jnp.float32)],
        compiler_params=pltpu.CompilerParams(vmem_limit_bytes=16 << 20),
        name="update",
    )(gathered, units, weight, moment, second)


def per_device(acts, cotangent, weight, moment, second):
    replicas, shards = lax.axis_size("rep"), lax.axis_size("col")
    rows, width = weight.shape
    far_first = slots(replicas)

    def sent(block, rep_step, col_step):
        route = []
        for r in range(replicas):
            for c in range(shards):
                target = peer(r, rep_step, replicas) * shards + peer(c, col_step, shards)
                route.append((r * shards + c, target))
        return lax.ppermute(block, ("rep", "col"), route)

    half = replicas // 2
    steps = [[(at, step) for at in range(replicas)] for step in range(shards)]
    runs = [steps[0][:half], steps[0][half:], steps[1]]
    runs += [sum(steps[at : at + 2], []) for at in range(2, shards, 2)]
    received = {}
    for run in runs:

        def block(index, run=run):
            at, col_step = run[index]
            return replica_at(at, replicas) * shards + shard_at(col_step, shards)

        codes = gradient_tiles(acts, cotangent, block, len(run), rows)
        for (at, col_step), code in zip(run, codes):
            if far_first[at] or col_step:
                code = sent(code, far_first[at], col_step)
            received[at, col_step] = code

    state = None
    for col_step in range(shards):
        codes = [received[at, col_step] for at in range(replicas)]
        shape = (replicas, rows, width)
        state = gram_tiles(codes, state, col_step, shape, shards)
    units, sums = state
    gathered = lax.all_to_all(sums, ("rep", "col"), 0, 0, tiled=True)
    return tuple(update_rows(gathered, units, weight, moment, second))


def solution(mesh):
    return jax.shard_map(
        per_device,
        mesh=mesh,
        in_specs=(
            P("rep", None),
            P("rep", "col"),
            P(("rep", "col"), None),
            P(("rep", "col"), None),
            P(("rep", "col"), None),
        ),
        out_specs=(
            P(("rep", "col"), None),
            P(("rep", "col"), None),
            P(("rep", "col"), None),
            P(("rep", "col"), None),
        ),
        check_vma=False,
    )
```
